128 devices in a mesh: seq: 8 (over x, core), head: 16 (over y, z).
Axes of the slice: x: 4, y: 4, z: 4, core: 2. Of those that a mesh axis runs over, the one named last changes fastest.
Arguments:
- tokens: bfloat16 [8192, 4096], P('seq'), may hold values from -16 to 16
- weights: bfloat16 [4096, 4, 4096], P(None, None, 'head'), may hold values from -0.09375 to 0.09375
- grad_output: bfloat16 [8192, 4096], P('seq', 'head'), may hold values from -6 to 6
- cluster: int32 [64], P('seq'), may hold values from 0 to 7, as said below
- slot: int32 [64], P('seq'), may hold values from 0 to 7, as said below
- pattern: int32 [8, 8, 8], P('seq'), may hold values from 0 to 1, as said below
Outputs:
- layer_out: bfloat16 [8192, 4096], P('seq', 'head')
- grad_tokens: bfloat16 [8192, 4096], P('seq', 'head')
- grad_weights: float32 [4096, 4, 4096], P('seq', None, 'head')
The draws below stay inside these ranges and needn't reach their ends.
Inputs may be any that keep to these rules, and one draw needn't show every extreme that they name: Every cluster holds exactly 8 blocks; the 8 blocks b with b // 8 equal go at most 2 times to one cluster, and some exactly 2 times. `slot`: numbers the blocks of each cluster 0 to 7 in the order of their block index. pattern[c, i, i] = 1 and pattern[c, i, j] = 0 for j > i.
All inputs are finite; a program needn't handle non-finite values.
Results may differ from the reference program's by a relative error of at most 0.019.
The reference program's roundings to bfloat16 on the way (of `projected`, `grad_attn`, `prob_low`, `attention`, `grad_score` and `grad_proj`) count: a program that leaves them out, or rounds other values in their place, can miss the bound.
Values may be sent and summed in bfloat16 or wider, within the bound.
No kernel may reach another device: no remote copies, remote signals or barrier semaphores. Data moves between devices by JAX's collectives and lax.ppermute only.
A program may use at most 192 MiB of HBM per device.

```python
import jax
import jax.numpy as jnp
from jax import lax

D = 4096
HEADS = 32
HD = 128
BLOCK = 128
CB = 8
HH = 4096
TOK_DEV = 1024
CLUSTERS = 8
BLOCKS = 64
TOKENS = 8192
N_SEQ = 8
N_HEAD = 16


def routing_tables(key):
    subkeys = jax.random.split(jax.random.fold_in(key, 11), 4)
    doubled = jax.random.randint(subkeys[0], (), 0, CLUSTERS).astype(jnp.int32)
    spread_vals = (doubled + 1 + jnp.arange(2 * CLUSTERS - 2, dtype=jnp.int32) % (CLUSTERS - 1)) % CLUSTERS
    chosen = jax.random.permutation(subkeys[1], spread_vals)[:CB - 2]
    offsets = jnp.concatenate([jnp.stack([doubled, doubled]), chosen]).astype(jnp.int32)
    relabel = jax.random.permutation(subkeys[2], CLUSTERS).astype(jnp.int32)
    ranking = jax.random.randint(subkeys[3], (CLUSTERS, CB), 0, 1 << 20) * CB + jnp.arange(CB, dtype=jnp.int32)[None, :]
    block_order = jnp.argsort(ranking, axis=1, stable=True)
    device = jnp.arange(CLUSTERS, dtype=jnp.int32)[:, None]
    cluster = relabel[(device + offsets[block_order]) % CLUSTERS].reshape(BLOCKS).astype(jnp.int32)
    same_owner = cluster[:, None] == cluster[None, :]
    before = jnp.arange(BLOCKS)[None, :] < jnp.arange(BLOCKS)[:, None]
    slot = jnp.sum(same_owner & before, axis=1).astype(jnp.int32)
    return (cluster, slot)


def draw_cluster(key, part):
    return routing_tables(key)[0]


def draw_slot(key, part):
    return routing_tables(key)[1]


def draw_pattern(key, part):
    subkeys = jax.random.split(jax.random.fold_in(key, 23), 2)
    density = jax.random.randint(subkeys[0], (CLUSTERS, 1, 1), 0, 5)
    coin_toss = jax.random.randint(subkeys[1], (CLUSTERS, CB, CB), 0, 4)
    lower = jnp.arange(CB)[None, :, None] > jnp.arange(CB)[None, None, :]
    diagonal = jnp.arange(CB)[None, :, None] == jnp.arange(CB)[None, None, :]
    return jnp.where(diagonal | lower & (coin_toss < density), 1, 0).astype(jnp.int32)


def draw_tokens(key, part):
    subkeys = jax.random.split(jax.random.fold_in(key, 5), 1)
    normal_base = jax.random.normal(subkeys[0], (TOKENS, D), jnp.float32)
    return jnp.clip(normal_base, -5.0, 5.0).astype(jnp.bfloat16)


def shard_levels(key, dims, cuts, low, largest):
    def one(dim, blocks):
        steps = jax.random.uniform(jax.random.fold_in(jax.random.fold_in(key, 6), dim), (blocks,), jnp.float32, low / len(cuts), largest / len(cuts))
        return jnp.repeat(jnp.exp(steps), dims[dim] // blocks).reshape((-1,) + (1,) * (len(dims) - dim - 1))

    factor_of = one(*cuts[0])
    for cut in cuts[1:]:
        factor_of = factor_of * one(*cut)
    return factor_of


def centred(stream_key, dims, deviation, reach, cuts=(), kind=jnp.bfloat16):
    level = shard_levels(stream_key, dims, cuts, -0.22, 0.18) if cuts else 1.0
    array = jax.random.normal(stream_key, dims, jnp.float32) * deviation * level
    return jnp.minimum(jnp.maximum(array, -reach), reach).astype(kind)


def setup_inputs(seed: int = 0) -> dict:
    key_list = jax.random.split(jax.random.key(seed), 7)
    tokens = draw_tokens(jax.random.fold_in(key_list[6], 71), 0)
    weights = centred(key_list[1], (D, 4, HH), D ** -0.5, 0.09375, ((2, 16),))
    grad_output = centred(key_list[2], (TOKENS, D), 1.0, 6.0, ((0, 8), (1, 16)))
    cluster = draw_cluster(jax.random.fold_in(key_list[6], 71), 0)
    slot = draw_slot(jax.random.fold_in(key_list[6], 71), 0)
    pattern = draw_pattern(jax.random.fold_in(key_list[6], 71), 0)
    return dict(tokens=tokens, weights=weights, grad_output=grad_output, cluster=cluster, slot=slot, pattern=pattern)


def rounded(value):
    return lax.optimization_barrier(value.astype(jnp.bfloat16)).astype(jnp.float32)


def cluster_mask(pattern_one, block_rows):
    blocks_in = pattern_one.shape[0]
    block_allowed = jnp.broadcast_to(pattern_one[:, None, :, None] == 1, (blocks_in, block_rows, blocks_in, block_rows))
    block_allowed = block_allowed.reshape(blocks_in * block_rows, blocks_in * block_rows)
    row_ids = lax.broadcasted_iota(jnp.int32, block_allowed.shape, 0)
    col_ids = lax.broadcasted_iota(jnp.int32, block_allowed.shape, 1)
    return block_allowed & (col_ids <= row_ids)


def attend_forward(queries, key_rows, values, allowed, factor):
    scores = jnp.einsum('ihd,jhd->hij', queries.astype(jnp.float32), key_rows.astype(jnp.float32)) * factor
    masked = jnp.where(allowed[None], scores, -1e30)
    row_max = jnp.max(masked, axis=2, keepdims=True)
    expo = jnp.where(allowed[None], jnp.exp(masked - row_max), 0.0)
    attn_prob = expo / jnp.sum(expo, axis=2, keepdims=True)
    prob_low = attn_prob.astype(jnp.bfloat16)
    attention = jnp.einsum('hij,jhd->ihd', prob_low.astype(jnp.float32), values.astype(jnp.float32)).astype(jnp.bfloat16)
    return attn_prob, prob_low, attention


def attend_backward(queries, key_rows, values, grad_attn, attn_prob, prob_low, factor):
    grad_prob = jnp.einsum('ihd,jhd->hij', grad_attn.astype(jnp.float32), values.astype(jnp.float32))
    row_delta = jnp.sum(attn_prob * grad_prob, axis=2, keepdims=True)
    grad_score = (attn_prob * (grad_prob - row_delta) * factor).astype(jnp.bfloat16).astype(jnp.float32)
    grad_q = jnp.einsum('hij,jhd->ihd', grad_score, key_rows.astype(jnp.float32)).astype(jnp.bfloat16)
    grad_k = jnp.einsum('hij,ihd->jhd', grad_score, queries.astype(jnp.float32)).astype(jnp.bfloat16)
    grad_v = jnp.einsum('hij,ihd->jhd', prob_low.astype(jnp.float32), grad_attn.astype(jnp.float32)).astype(jnp.bfloat16)
    return grad_q, grad_k, grad_v


def reference(tokens, weights, grad_output, cluster, slot, pattern):
    factor = HD ** -0.5
    projected = jnp.einsum('td,dpc->tpc', tokens.astype(jnp.float32), weights[:, :3, :].astype(jnp.float32)).astype(jnp.bfloat16)
    grad_attn = jnp.dot(grad_output, weights[:, 3, :], preferred_element_type=jnp.float32).astype(jnp.bfloat16)
    packed = jnp.concatenate([projected, grad_attn[:, None, :]], axis=1)
    destination = (cluster.astype(jnp.int32) * CB + slot.astype(jnp.int32)).astype(jnp.int32)
    source = jnp.zeros((BLOCKS,), jnp.int32).at[destination].set(jnp.arange(BLOCKS, dtype=jnp.int32))
    grouped = packed.reshape(BLOCKS, BLOCK, 4, HH)[source].reshape(CLUSTERS, CB * BLOCK, 4, HEADS, HD)

    def one_cluster(operands):
        rows_here, pattern_one = operands
        allowed = cluster_mask(pattern_one, BLOCK)
        queries = rows_here[:, 0]
        key_rows = rows_here[:, 1]
        values = rows_here[:, 2]
        grad_rows = rows_here[:, 3]
        attn_prob, prob_low, attention = attend_forward(queries, key_rows, values, allowed, factor)
        grad_q, grad_k, grad_v = attend_backward(queries, key_rows, values, grad_rows, attn_prob, prob_low, factor)
        return jnp.stack([attention, grad_q, grad_k, grad_v], axis=1)

    results = lax.map(one_cluster, (grouped, pattern))
    results = results.reshape(BLOCKS, BLOCK, 4, HH)[destination].reshape(TOKENS, 4, HH)
    attention = results[:, 0]
    grad_proj = results[:, 1:]
    group_width = HH // N_HEAD
    layer_out = jnp.zeros((TOKENS, D), jnp.float32)
    grad_tokens = jnp.zeros((TOKENS, D), jnp.float32)
    for group in range(N_HEAD):
        low = group * group_width
        high = low + group_width
        partial_value = jnp.dot(attention[:, low:high], weights[:, 3, low:high].T, preferred_element_type=jnp.float32)
        layer_out = layer_out + rounded(partial_value)
        partial_value = jnp.einsum('tpc,dpc->td', grad_proj[:, :, low:high].astype(jnp.float32), weights[:, :3, low:high].astype(jnp.float32))
        grad_tokens = grad_tokens + rounded(partial_value)
    grad_weights = jnp.zeros((D, 4, HH), jnp.float32)
    for shard in range(N_SEQ):
        low = shard * TOK_DEV
        high = low + TOK_DEV
        part_qkv = jnp.einsum('td,tpc->dpc', tokens[low:high].astype(jnp.float32), grad_proj[low:high].astype(jnp.float32))
        part_out = jnp.einsum('td,tc->dc', grad_output[low:high].astype(jnp.float32), attention[low:high].astype(jnp.float32))
        weight_part = jnp.concatenate([part_qkv, part_out[:, None, :]], axis=1)
        grad_weights = grad_weights + rounded(weight_part)
    return layer_out.astype(jnp.bfloat16), grad_tokens.astype(jnp.bfloat16), grad_weights
```

```python
import jax
import jax.numpy as jnp
from jax import lax
from jax.experimental import pallas as pl
from jax.experimental.pallas import tpu as pltpu
from jax.sharding import PartitionSpec as P

HD = 128
BLOCK = 128
CB = 8
CAP = 2
F32 = jnp.float32
BF16 = jnp.bfloat16
VMEM_LIMIT = 60 * 1024 * 1024


def y_shift(d):
    return [(h, ((h // 4 + d) % 4) * 4 + h % 4) for h in range(16)]


def z_shift(d):
    return [(h, (h // 4) * 4 + (h % 4 + d) % 4) for h in range(16)]


def x_shift(d):
    return [(s, (s + 2 * d) % 8) for s in range(8)]


CORE_SWAP = [(s, s ^ 1) for s in range(8)]


def gather_axis(own, shift):
    half = own.shape[0] // 2
    below = lax.ppermute(own, "head", shift(1))
    above = lax.ppermute(own, "head", shift(-1))
    far_a = lax.ppermute(below[:half], "head", shift(1))
    far_b = lax.ppermute(above[half:], "head", shift(-1))
    return own, below, jnp.concatenate([far_a, far_b], axis=0), above


def gather_plane(own, first, second):
    near = gather_axis(own, first)
    return gather_axis(jnp.stack(near, axis=0), second)


def scatter_axis(chunks, axis, shift, out_type):
    half = chunks[2].shape[0] // 2
    far_a = lax.ppermute(chunks[2][:half], axis, shift(1))
    far_b = lax.ppermute(chunks[2][half:], axis, shift(-1))
    up = jnp.concatenate(
        [(chunks[1][:half].astype(F32) + far_a.astype(F32)).astype(BF16), chunks[1][half:]], axis=0
    )
    down = jnp.concatenate(
        [chunks[3][:half], (chunks[3][half:].astype(F32) + far_b.astype(F32)).astype(BF16)], axis=0
    )
    from_below = lax.ppermute(up, axis, shift(1))
    from_above = lax.ppermute(down, axis, shift(-1))
    total = chunks[0].astype(F32) + from_below.astype(F32) + from_above.astype(F32)
    return total.astype(out_type)


def scatter_plane(parts, first, second):
    mid = scatter_axis([parts[r] for r in range(4)], "head", first, BF16)
    return scatter_axis([mid[r] for r in range(4)], "head", second, BF16)


def scatter_seq(parts):
    other = lax.ppermute(parts[1], "seq", CORE_SWAP)
    chip = (parts[0].astype(F32) + other.astype(F32)).astype(BF16)
    return scatter_axis([chip[r] for r in range(4)], "seq", x_shift, F32)


def call(kernel, name, grid, prefetch, in_specs, out_specs, out_shape, scratch, flops, moved):
    return pl.pallas_call(
        kernel,
        name=name,
        grid_spec=pltpu.PrefetchScalarGridSpec(
            num_scalar_prefetch=prefetch,
            grid=grid,
            in_specs=in_specs,
            out_specs=out_specs,
            scratch_shapes=scratch,
        ),
        out_shape=out_shape,
        compiler_params=pltpu.CompilerParams(vmem_limit_bytes=VMEM_LIMIT),
        cost_estimate=pl.CostEstimate(flops=flops, bytes_accessed=moved, transcendentals=0),
    )


def rows(b):
    return pl.ds(b * BLOCK, BLOCK)


def project(entry, tokens, weights):
    tok, dim = tokens.shape
    wide = 768
    steps = 4
    depth = dim // steps

    def kernel(entry_ref, tok_ref, w_ref, out_ref, acc_ref):
        k = pl.program_id(0)
        part = jnp.dot(tok_ref[...], w_ref[...], preferred_element_type=F32)

        @pl.when(k == 0)
        def _():
            acc_ref[...] = part

        @pl.when((k > 0) & (k < steps - 1))
        def _():
            acc_ref[...] += part

        @pl.when(k == steps - 1)
        def _():
            acc_ref[...] += part
            for b in range(tok // BLOCK):
                for p in range(3):
                    out_ref[entry_ref[b], p] = acc_ref[rows(b), p * 256 : (p + 1) * 256].astype(BF16)

    return call(
        kernel,
        "project",
        (steps,),
        1,
        [
            pl.BlockSpec((tok, depth), lambda k, e: (0, k)),
            pl.BlockSpec((depth, wide), lambda k, e: (k, 0)),
        ],
        pl.BlockSpec((16, 3, BLOCK, 256), lambda k, e: (0, 0, 0, 0)),
        jax.ShapeDtypeStruct((16, 3, BLOCK, 256), BF16),
        [pltpu.VMEM((tok, wide), F32)],
        2 * tok * dim * wide,
        2 * (tok * dim + dim * wide + tok * wide),
    )(entry, tokens, weights)


def attn_cotangent(entry, where, half_a, half_b, weights):
    def kernel(entry_ref, where_ref, *refs):
        a_refs, b_refs, w_ref, out_ref, acc_ref = refs[:4], refs[4:8], refs[8], refs[9], refs[10]
        i = pl.program_id(0)

        @pl.when(i == 0)
        def _():
            acc_ref[...] = jnp.zeros_like(acc_ref)

        for j in range(4):
            da = pl.multiple_of(where_ref[i * 4 + j] * 256, 256)
            db = pl.multiple_of(where_ref[j * 4 + i] * 256, 256)
            acc_ref[:512] += jnp.dot(
                a_refs[j][0], w_ref[pl.ds(da, 256), :], preferred_element_type=F32
            )
            acc_ref[512:] += jnp.dot(
                b_refs[j][0], w_ref[pl.ds(db, 256), :], preferred_element_type=F32
            )

        @pl.when(i == 3)
        def _():
            for b in range(8):
                out_ref[entry_ref[b]] = acc_ref[rows(b), :].astype(BF16)

    piece = pl.BlockSpec((1, 512, 256), lambda i, e, w: (i, 0, 0))
    return call(
        kernel,
        "attn_cotangent",
        (4,),
        2,
        [piece] * 8 + [pl.BlockSpec((4096, 256), lambda i, e, w: (0, 3))],
        pl.BlockSpec((16, BLOCK, 256), lambda i, e, w: (0, 0, 0)),
        jax.ShapeDtypeStruct((16, BLOCK, 256), BF16),
        [pltpu.VMEM((1024, 256), F32)],
        2 * 1024 * 4096 * 256,
        2 * (1024 * 4096 + 4096 * 256 + 1024 * 256),
    )(entry, where, *half_a, *half_b, weights)


def probabilities(i, q, keys, pattern_ref, factor):
    width = (i + 1) * BLOCK
    scores = (
        lax.dot_general(q, keys[:width, :], (((1,), (1,)), ((), ())), preferred_element_type=F32)
        * factor
    )
    row_ids = lax.broadcasted_iota(jnp.int32, (BLOCK, BLOCK), 0)
    col_ids = lax.broadcasted_iota(jnp.int32, (BLOCK, BLOCK), 1)
    pieces = []
    for j in range(i + 1):
        piece = scores[:, j * BLOCK : (j + 1) * BLOCK]
        if j == i:
            pieces.append(jnp.where(col_ids <= row_ids, piece, -1e30))
        else:
            pieces.append(jnp.where(pattern_ref[i * CB + j] == 1, piece, -1e30))
    masked = jnp.concatenate(pieces, axis=1) if i else pieces[0]
    expo = jnp.exp(masked - jnp.max(masked, axis=1, keepdims=True))
    return expo / jnp.sum(expo, axis=1, keepdims=True)


def attend_forward(entry, pattern, qkv):
    factor = HD ** (-0.5)

    def kernel(entry_ref, pattern_ref, qkv_ref, out_ref, k_ref, v_ref):
        for s in range(CB):
            k_ref[rows(s), :] = qkv_ref[entry_ref[s], 1]
            v_ref[rows(s), :] = qkv_ref[entry_ref[s], 2]
        for i in range(CB):
            prob = probabilities(i, qkv_ref[entry_ref[i], 0], k_ref, pattern_ref, factor)
            out_ref[entry_ref[i]] = jnp.dot(
                prob.astype(BF16), v_ref[: (i + 1) * BLOCK, :], preferred_element_type=F32
            ).astype(BF16)

    return call(
        kernel,
        "attend_forward",
        (2,),
        2,
        [pl.BlockSpec((16, 3, BLOCK, HD), lambda h, e, p: (0, 0, 0, h))],
        pl.BlockSpec((16, BLOCK, HD), lambda h, e, p: (0, 0, h)),
        jax.ShapeDtypeStruct((16, BLOCK, 256), BF16),
        [pltpu.VMEM((1024, HD), BF16), pltpu.VMEM((1024, HD), BF16)],
        2 * 2 * 2 * 1024 * 1024 * 128,
        2 * (16 * BLOCK * 1024),
    )(entry, pattern, qkv)


def attend_backward(entry, pattern, qkv, grad):
    factor = HD ** (-0.5)

    def kernel(entry_ref, pattern_ref, qkv_ref, g_ref, out_ref, k_ref, v_ref, dk_ref, dv_ref):
        for s in range(CB):
            k_ref[rows(s), :] = qkv_ref[entry_ref[s], 1]
            v_ref[rows(s), :] = qkv_ref[entry_ref[s], 2]
        dk_ref[...] = jnp.zeros_like(dk_ref)
        dv_ref[...] = jnp.zeros_like(dv_ref)
        for i in range(CB):
            width = (i + 1) * BLOCK
            q = qkv_ref[entry_ref[i], 0]
            g = g_ref[entry_ref[i]]
            prob = probabilities(i, q, k_ref, pattern_ref, factor)
            grad_prob = lax.dot_general(
                g, v_ref[:width, :], (((1,), (1,)), ((), ())), preferred_element_type=F32
            )
            row_delta = jnp.sum(prob * grad_prob, axis=1, keepdims=True)
            grad_score = (prob * (grad_prob - row_delta) * factor).astype(BF16)
            out_ref[entry_ref[i], 0] = jnp.dot(
                grad_score, k_ref[:width, :], preferred_element_type=F32
            ).astype(BF16)
            dk_ref[:width, :] += lax.dot_general(
                grad_score, q, (((0,), (0,)), ((), ())), preferred_element_type=F32
            )
            dv_ref[:width, :] += lax.dot_general(
                prob.astype(BF16), g, (((0,), (0,)), ((), ())), preferred_element_type=F32
            )
        for s in range(CB):
            out_ref[entry_ref[s], 1] = dk_ref[rows(s), :].astype(BF16)
            out_ref[entry_ref[s], 2] = dv_ref[rows(s), :].astype(BF16)

    return call(
        kernel,
        "attend_backward",
        (2,),
        2,
        [
            pl.BlockSpec((16, 3, BLOCK, HD), lambda h, e, p: (0, 0, 0, h)),
            pl.BlockSpec((16, BLOCK, HD), lambda h, e, p: (0, 0, h)),
        ],
        pl.BlockSpec((16, 3, BLOCK, HD), lambda h, e, p: (0, 0, 0, h)),
        jax.ShapeDtypeStruct((16, 3, BLOCK, 256), BF16),
        [
            pltpu.VMEM((1024, HD), BF16),
            pltpu.VMEM((1024, HD), BF16),
            pltpu.VMEM((1024, HD), F32),
            pltpu.VMEM((1024, HD), F32),
        ],
        2 * 5 * 2 * 1024 * 1024 * 128,
        2 * (16 * BLOCK * 256 * 7),
    )(entry, pattern, qkv, grad)


def output_parts(entry, where, home, weights, count, column):
    wide = count * 256

    def kernel(entry_ref, where_ref, home_ref, w_ref, a_ref, b_ref, lhs_ref):
        @pl.when((pl.program_id(0) == 0) & (pl.program_id(1) == 0))
        def _():
            for b in range(8):
                for p in range(count):
                    lhs_ref[rows(b), p * 256 : (p + 1) * 256] = home_ref[entry_ref[b], p]

        part = lax.dot_general(
            lhs_ref[...], w_ref[...], (((1,), (1,)), ((), ())), preferred_element_type=F32
        ).astype(BF16)
        a_ref[0, 0] = part[:512]
        b_ref[0, 0] = part[512:]

    shape = jax.ShapeDtypeStruct((4, 4, 512, 256), BF16)
    return call(
        kernel,
        f"output_parts_{count}",
        (4, 4),
        2,
        [
            pl.BlockSpec((16, count, BLOCK, 256), lambda i, j, e, w: (0, 0, 0, 0)),
            pl.BlockSpec((256, wide), lambda i, j, e, w: (w[i * 4 + j], column)),
        ],
        [
            pl.BlockSpec((1, 1, 512, 256), lambda i, j, e, w: (i, j, 0, 0)),
            pl.BlockSpec((1, 1, 512, 256), lambda i, j, e, w: (j, i, 0, 0)),
        ],
        [shape, shape],
        [pltpu.VMEM((1024, wide), BF16)],
        2 * 1024 * 4096 * wide,
        2 * (16 * BLOCK * wide + 4096 * wide + 1024 * 4096),
    )(entry, where, home, weights)


def weight_grad_qkv(entry, place, tokens, home):
    def kernel(entry_ref, place_ref, tok_ref, home_ref, out_ref, rhs_ref):
        @pl.when(pl.program_id(0) == 0)
        def _():
            for b in range(8):
                for p in range(3):
                    rhs_ref[rows(b), p * 256 : (p + 1) * 256] = home_ref[entry_ref[b], p]

        out_ref[0, 0] = lax.dot_general(
            tok_ref[...], rhs_ref[...], (((0,), (0,)), ((), ())), preferred_element_type=F32
        ).astype(BF16)

    return call(
        kernel,
        "weight_grad_qkv",
        (8,),
        2,
        [
            pl.BlockSpec((1024, 512), lambda i, e, s: (0, i)),
            pl.BlockSpec((16, 3, BLOCK, 256), lambda i, e, s: (0, 0, 0, 0)),
        ],
        pl.BlockSpec((1, 1, 512, 768), lambda i, e, s: (s[i] // 4, s[i] % 4, 0, 0)),
        jax.ShapeDtypeStruct((2, 4, 512, 768), BF16),
        [pltpu.VMEM((1024, 768), BF16)],
        2 * 1024 * 4096 * 768,
        2 * (1024 * 4096 + 16 * BLOCK * 768 + 4096 * 768),
    )(entry, place, tokens, home)


def weight_grad_out(entry, where, place, half_a, half_b, home):
    def kernel(entry_ref, where_ref, place_ref, *refs):
        a_refs, b_refs, home_ref, out_ref, rhs_ref = refs[:4], refs[4:8], refs[8], refs[9], refs[10]
        for b in range(8):
            rhs_ref[rows(b), :] = home_ref[entry_ref[b], 0]

        for i in range(4):
            for j in range(4):
                d = where_ref[i * 4 + j]
                s = place_ref[d // 2]
                part = lax.dot_general(
                    a_refs[j][i], rhs_ref[:512], (((0,), (0,)), ((), ())), preferred_element_type=F32
                )
                part += lax.dot_general(
                    b_refs[i][j], rhs_ref[512:], (((0,), (0,)), ((), ())), preferred_element_type=F32
                )
                low = pl.multiple_of((d % 2) * 256, 256)
                out_ref[s // 4, s % 4, pl.ds(low, 256), :] = part.astype(BF16)

    piece = pl.BlockSpec((4, 512, 256), lambda i, e, w, s: (0, 0, 0))
    return call(
        kernel,
        "weight_grad_out",
        (1,),
        3,
        [piece] * 8 + [pl.BlockSpec((16, 1, BLOCK, 256), lambda i, e, w, s: (0, 0, 0, 0))],
        pl.BlockSpec((2, 4, 512, 256), lambda i, e, w, s: (0, 0, 0, 0)),
        jax.ShapeDtypeStruct((2, 4, 512, 256), BF16),
        [pltpu.VMEM((1024, 256), BF16)],
        2 * 1024 * 4096 * 256,
        2 * (1024 * 4096 + 16 * BLOCK * 256 + 4096 * 256),
    )(entry, where, place, *half_a, *half_b, home)


def to_seq(array):
    return lax.all_to_all(array, "seq", split_axis=0, concat_axis=0, tiled=True)


def shards(tokens, weights, grad_output, cluster, slot, pattern):
    block_count = cluster.shape[0]
    entries = 16
    head = lax.axis_index("head")
    seq = lax.axis_index("seq")
    y, z = head // 4, head % 4
    near = jnp.arange(4, dtype=jnp.int32)
    source = (((y - near) % 4)[:, None] * 4 + ((z - near) % 4)[None, :]).reshape(16)
    target = (((y + near) % 4)[:, None] * 4 + ((z + near) % 4)[None, :]).reshape(16)
    owner = jnp.arange(8, dtype=jnp.int32)
    place = ((owner % 2 + seq) % 2) * 4 + (owner // 2 - seq // 2) % 4

    same_owner = cluster[:, None] == cluster[None, :]
    before = jnp.arange(block_count)[None, :] < jnp.arange(block_count)[:, None]
    block_rank = jnp.sum((same_owner & before).astype(jnp.int32), axis=1)
    home_entry = cluster * CAP + block_rank
    picker = home_entry[:, None] == jnp.arange(entries, dtype=jnp.int32)[None, :]
    slot_tags = (jnp.sum(jnp.where(picker, slot[:, None] + 1, 0), axis=0) - 1).reshape(8, CAP)
    tags_in = to_seq(slot_tags).reshape(entries)
    arranger = jnp.arange(CB, dtype=jnp.int32)[:, None] == tags_in[None, :]
    slot_entry = jnp.sum(
        jnp.where(arranger, jnp.arange(entries, dtype=jnp.int32)[None, :], 0), axis=1
    )
    pattern = pattern.reshape(CB * CB)

    half_a = gather_plane(grad_output[:512], y_shift, z_shift)
    half_b = gather_plane(grad_output[512:], z_shift, y_shift)

    flat = weights.reshape(weights.shape[0], 4 * weights.shape[2])
    qkv = to_seq(project(home_entry, tokens, flat))
    attention = attend_forward(slot_entry, pattern, qkv)
    attention = to_seq(attention).reshape(16, 1, BLOCK, 256)

    grad_attn = to_seq(attn_cotangent(home_entry, source, half_a, half_b, flat))
    out_a, out_b = output_parts(home_entry, target, attention, flat, 1, 3)
    out_a = scatter_plane(out_a, y_shift, z_shift)
    out_b = scatter_plane(out_b, z_shift, y_shift)
    layer_out = jnp.concatenate([out_a, out_b], axis=0)
    grad_w3 = scatter_seq(weight_grad_out(home_entry, source, place, half_a, half_b, attention))

    grads = to_seq(attend_backward(slot_entry, pattern, qkv, grad_attn))
    tok_a, tok_b = output_parts(home_entry, target, grads, flat, 3, 0)
    tok_a = scatter_plane(tok_a, y_shift, z_shift)
    tok_b = scatter_plane(tok_b, z_shift, y_shift)
    grad_tokens = jnp.concatenate([tok_a, tok_b], axis=0)
    grad_wqkv = scatter_seq(weight_grad_qkv(home_entry, place, tokens, grads))
    grad_weights = jnp.concatenate([grad_wqkv, grad_w3], axis=1).reshape(512, 4, 256)
    return (layer_out, grad_tokens, grad_weights)


def solution(mesh):
    in_specs = (
        P("seq", None),
        P(None, None, "head"),
        P("seq", "head"),
        P("seq"),
        P("seq"),
        P("seq", None, None),
    )
    out_specs = (P("seq", "head"), P("seq", "head"), P("seq", None, "head"))
    return jax.shard_map(shards, mesh=mesh, in_specs=in_specs, out_specs=out_specs, check_vma=False)
```

```python
import jax
import jax.numpy as jnp
from jax import lax
from jax.experimental import pallas as pl
from jax.experimental.pallas import tpu as pltpu
from jax.sharding import PartitionSpec as P

HD = 128
BLOCK = 128
CB = 8
CAP = 2
F32 = jnp.float32
BF16 = jnp.bfloat16
VMEM_LIMIT = 60 * 1024 * 1024


def pairing(axis, step):
    pairs = []
    for me in range(128):
        x, core, y, z = me // 32, me // 16 % 2, me // 4 % 4, me % 4
        flip = (1, 3)[core ^ step]
        if axis == "x":
            x ^= flip
        elif axis == "y":
            y ^= flip
        else:
            z ^= flip
        pairs.append((me, ((x * 2 + core) * 4 + y) * 4 + z))
    return pairs


def swap(array, axis, step):
    return lax.ppermute(array, ("seq", "head"), pairing(axis, step))


def gather_plane(own, first, second):
    near = jnp.stack([own, swap(own, first, 0)], axis=0)
    line = jnp.concatenate([near, swap(near, first, 1)], axis=0)
    near = jnp.stack([line, swap(line, second, 0)], axis=0)
    return near, swap(near, second, 1)


def added(a, b, out_type):
    return (a.astype(F32) + b.astype(F32)).astype(out_type)


def scatter_axis(near, far, axis, out_type):
    far = swap(far, axis, 1)
    other = swap(added(near[1], far[1], BF16), axis, 0)
    return (near[0].astype(F32) + far[0].astype(F32) + other.astype(F32)).astype(out_type)


def scatter_plane(near, far, first, second):
    line = scatter_axis(near, far, first, BF16)
    return scatter_axis(line[:2], line[2:], second, BF16)


def scatter_seq(parts):
    other = lax.ppermute(parts[1], "seq", [(s, s ^ 1) for s in range(8)])
    chip = added(parts[0], other, BF16)
    return scatter_axis(chip[:2], chip[2:], "x", F32)


def call(
    kernel, name, grid, prefetch, in_specs, out_specs, out_shape, scratch, flops, moved, aliases=None
):
    return pl.pallas_call(
        kernel,
        name=name,
        grid_spec=pltpu.PrefetchScalarGridSpec(
            num_scalar_prefetch=prefetch,
            grid=grid,
            in_specs=in_specs,
            out_specs=out_specs,
            scratch_shapes=scratch,
        ),
        out_shape=out_shape,
        input_output_aliases=aliases or {},
        compiler_params=pltpu.CompilerParams(vmem_limit_bytes=VMEM_LIMIT),
        cost_estimate=pl.CostEstimate(flops=flops, bytes_accessed=moved, transcendentals=0),
    )


def rows(b):
    return pl.ds(b * BLOCK, BLOCK)


def project(entry, tokens, weights):
    tok, dim = tokens.shape

    def kernel(entry_ref, tok_ref, w_ref, out_ref):
        p = pl.program_id(0)
        part = jnp.dot(tok_ref[...], w_ref[...], preferred_element_type=F32).astype(BF16)
        for b in range(tok // BLOCK):
            out_ref[entry_ref[b], p] = part[b * BLOCK : (b + 1) * BLOCK]

    return call(
        kernel,
        "project",
        (3,),
        1,
        [
            pl.BlockSpec((tok, dim), lambda p, e: (0, 0)),
            pl.BlockSpec((dim, 256), lambda p, e: (0, p)),
        ],
        pl.BlockSpec((16, 3, BLOCK, 256), lambda p, e: (0, 0, 0, 0)),
        jax.ShapeDtypeStruct((16, 3, BLOCK, 256), BF16),
        [],
        2 * tok * dim * 768,
        2 * (tok * dim + dim * 768 + tok * 768),
    )(entry, tokens, weights)


def attn_cotangent(entry, where, half_a, half_b, weights):
    def kernel(entry_ref, where_ref, na_ref, fa_ref, nb_ref, fb_ref, w_ref, out_ref, acc_ref):
        i = pl.program_id(0)

        @pl.when(i == 0)
        def _():
            acc_ref[...] = jnp.zeros_like(acc_ref)

        for low, near_ref, far_ref, across in ((0, na_ref, fa_ref, False), (512, nb_ref, fb_ref, True)):
            lhs = jnp.concatenate(
                [near_ref[0, 0], near_ref[1, 0], far_ref[0, 0], far_ref[1, 0]], axis=1
            )
            picked = []
            for j in range(4):
                d = where_ref[j * 4 + i] if across else where_ref[i * 4 + j]
                picked.append(w_ref[pl.ds(pl.multiple_of(d * 256, 256), 256), :])
            acc_ref[low : low + 512] += jnp.dot(
                lhs, jnp.concatenate(picked, axis=0), preferred_element_type=F32
            )

        @pl.when(i == 3)
        def _():
            for b in range(8):
                out_ref[entry_ref[b]] = acc_ref[rows(b), :].astype(BF16)

    piece = pl.BlockSpec((2, 1, 512, 256), lambda i, e, w: (0, i, 0, 0))
    return call(
        kernel,
        "attn_cotangent",
        (4,),
        2,
        [piece] * 4 + [pl.BlockSpec((4096, 256), lambda i, e, w: (0, 3))],
        pl.BlockSpec((16, BLOCK, 256), lambda i, e, w: (0, 0, 0)),
        jax.ShapeDtypeStruct((16, BLOCK, 256), BF16),
        [pltpu.VMEM((1024, 256), F32)],
        2 * 1024 * 4096 * 256,
        2 * (1024 * 4096 + 4096 * 256 + 1024 * 256),
    )(entry, where, *half_a, *half_b, weights)


def probabilities(i, q, keys, pattern_ref, factor):
    width = (i + 1) * BLOCK
    scores = (
        lax.dot_general(q, keys[:width, :], (((1,), (1,)), ((), ())), preferred_element_type=F32)
        * factor
    )
    row_ids = lax.broadcasted_iota(jnp.int32, (BLOCK, BLOCK), 0)
    col_ids = lax.broadcasted_iota(jnp.int32, (BLOCK, BLOCK), 1)
    pieces = []
    for j in range(i + 1):
        piece = scores[:, j * BLOCK : (j + 1) * BLOCK]
        if j == i:
            pieces.append(jnp.where(col_ids <= row_ids, piece, -1e30))
        else:
            pieces.append(jnp.where(pattern_ref[i * CB + j] == 1, piece, -1e30))
    masked = jnp.concatenate(pieces, axis=1) if i else pieces[0]
    expo = jnp.exp(masked - jnp.max(masked, axis=1, keepdims=True))
    return expo / jnp.sum(expo, axis=1, keepdims=True)


def attend_forward(entry, pattern, qkv):
    factor = HD ** (-0.5)

    def kernel(entry_ref, pattern_ref, qkv_ref, out_ref, k_ref, v_ref):
        for s in range(CB):
            k_ref[rows(s), :] = qkv_ref[entry_ref[s], 1]
            v_ref[rows(s), :] = qkv_ref[entry_ref[s], 2]
        for i in range(CB):
            prob = probabilities(i, qkv_ref[entry_ref[i], 0], k_ref, pattern_ref, factor)
            out_ref[entry_ref[i]] = jnp.dot(
                prob.astype(BF16), v_ref[: (i + 1) * BLOCK, :], preferred_element_type=F32
            ).astype(BF16)

    return call(
        kernel,
        "attend_forward",
        (2,),
        2,
        [pl.BlockSpec((16, 3, BLOCK, HD), lambda h, e, p: (0, 0, 0, h))],
        pl.BlockSpec((16, BLOCK, HD), lambda h, e, p: (0, 0, h)),
        jax.ShapeDtypeStruct((16, BLOCK, 256), BF16),
        [pltpu.VMEM((1024, HD), BF16), pltpu.VMEM((1024, HD), BF16)],
        2 * 2 * 2 * 1024 * 1024 * 128,
        2 * (16 * BLOCK * 1024),
    )(entry, pattern, qkv)


def attend_backward(entry, pattern, qkv, grad):
    factor = HD ** (-0.5)

    def kernel(entry_ref, pattern_ref, qkv_ref, g_ref, out_ref, k_ref, v_ref, dk_ref, dv_ref):
        for s in range(CB):
            k_ref[rows(s), :] = qkv_ref[entry_ref[s], 1]
            v_ref[rows(s), :] = qkv_ref[entry_ref[s], 2]
        dk_ref[...] = jnp.zeros_like(dk_ref)
        dv_ref[...] = jnp.zeros_like(dv_ref)
        for i in range(CB):
            width = (i + 1) * BLOCK
            q = qkv_ref[entry_ref[i], 0]
            g = g_ref[entry_ref[i]]
            prob = probabilities(i, q, k_ref, pattern_ref, factor)
            grad_prob = lax.dot_general(
                g, v_ref[:width, :], (((1,), (1,)), ((), ())), preferred_element_type=F32
            )
            row_delta = jnp.sum(prob * grad_prob, axis=1, keepdims=True)
            grad_score = (prob * (grad_prob - row_delta) * factor).astype(BF16)
            out_ref[entry_ref[i], 0] = jnp.dot(
                grad_score, k_ref[:width, :], preferred_element_type=F32
            ).astype(BF16)
            dk_ref[:width, :] += lax.dot_general(
                grad_score, q, (((0,), (0,)), ((), ())), preferred_element_type=F32
            )
            dv_ref[:width, :] += lax.dot_general(
                prob.astype(BF16), g, (((0,), (0,)), ((), ())), preferred_element_type=F32
            )
        for s in range(CB):
            out_ref[entry_ref[s], 1] = dk_ref[rows(s), :].astype(BF16)
            out_ref[entry_ref[s], 2] = dv_ref[rows(s), :].astype(BF16)

    return call(
        kernel,
        "attend_backward",
        (2,),
        2,
        [
            pl.BlockSpec((16, 3, BLOCK, HD), lambda h, e, p: (0, 0, 0, h)),
            pl.BlockSpec((16, BLOCK, HD), lambda h, e, p: (0, 0, h)),
        ],
        pl.BlockSpec((16, 3, BLOCK, HD), lambda h, e, p: (0, 0, 0, h)),
        jax.ShapeDtypeStruct((16, 3, BLOCK, 256), BF16),
        [
            pltpu.VMEM((1024, HD), BF16),
            pltpu.VMEM((1024, HD), BF16),
            pltpu.VMEM((1024, HD), F32),
            pltpu.VMEM((1024, HD), F32),
        ],
        2 * 5 * 2 * 1024 * 1024 * 128,
        2 * (16 * BLOCK * 256 * 7),
    )(entry, pattern, qkv, grad)


def output_parts(entry, where, home, weights, count, column, far):
    wide = count * 256

    def kernel(entry_ref, where_ref, home_ref, w_ref, a_ref, b_ref, lhs_ref):
        i = pl.program_id(0)

        @pl.when(i == 0)
        def _():
            for b in range(8):
                for p in range(count):
                    lhs_ref[rows(b), p * 256 : (p + 1) * 256] = home_ref[entry_ref[b], p]

        outer = i + 2 * far
        for j in range(4):
            for low, part_ref, d in (
                (0, a_ref, where_ref[outer * 4 + j]),
                (512, b_ref, where_ref[j * 4 + outer]),
            ):
                part_ref[0, j] = lax.dot_general(
                    lhs_ref[low : low + 512],
                    w_ref[pl.ds(pl.multiple_of(d * 256, 256), 256), :],
                    (((1,), (1,)), ((), ())),
                    preferred_element_type=F32,
                ).astype(BF16)

    shape = jax.ShapeDtypeStruct((2, 4, 512, 256), BF16)
    return call(
        kernel,
        f"output_parts_{count}_{far}",
        (2,),
        2,
        [
            pl.BlockSpec((16, count, BLOCK, 256), lambda i, e, w: (0, 0, 0, 0)),
            pl.BlockSpec((4096, wide), lambda i, e, w: (0, column)),
        ],
        [pl.BlockSpec((1, 4, 512, 256), lambda i, e, w: (i, 0, 0, 0))] * 2,
        [shape, shape],
        [pltpu.VMEM((1024, wide), BF16)],
        1024 * 4096 * wide,
        2 * (16 * BLOCK * wide + 4096 * wide + 512 * 4096),
    )(entry, where, home, weights)


def turned(rows_ref, entry_ref, home_ref, count):
    for b in range(8):
        for p in range(count):
            rows_ref[p * 256 : (p + 1) * 256, rows(b)] = home_ref[entry_ref[b], p].T


def weight_grad_qkv(entry, place, tokens, home, target):
    def kernel(entry_ref, place_ref, tok_ref, home_ref, target_ref, out_ref, lhs_ref):
        @pl.when(pl.program_id(0) == 0)
        def _():
            turned(lhs_ref, entry_ref, home_ref, 3)

        out_ref[0, 0] = jnp.dot(lhs_ref[...], tok_ref[...], preferred_element_type=F32).astype(BF16)

    return call(
        kernel,
        "weight_grad_qkv",
        (8,),
        2,
        [
            pl.BlockSpec((1024, 512), lambda i, e, s: (0, i)),
            pl.BlockSpec((16, 3, BLOCK, 256), lambda i, e, s: (0, 0, 0, 0)),
            pl.BlockSpec(memory_space=pl.ANY),
        ],
        pl.BlockSpec((1, 1, 768, 512), lambda i, e, s: (s[i] // 4, s[i] % 4, 0, 0)),
        jax.ShapeDtypeStruct((2, 4, 1024, 512), BF16),
        [pltpu.VMEM((768, 1024), BF16)],
        2 * 1024 * 4096 * 768,
        2 * (1024 * 4096 + 16 * BLOCK * 768 + 4096 * 768),
        {4: 0},
    )(entry, place, tokens, home, target)


def weight_grad_out(entry, where, place, half_a, half_b, home):
    def kernel(
        entry_ref, where_ref, place_ref, na_ref, fa_ref, nb_ref, fb_ref, home_ref, out_ref, lhs_ref
    ):
        turned(lhs_ref, entry_ref, home_ref, 1)
        for i in range(4):
            for j in range(4):
                d = where_ref[i * 4 + j]
                s = place_ref[d // 2]
                a_ref = (na_ref, fa_ref)[j // 2]
                b_ref = (nb_ref, fb_ref)[i // 2]
                part = jnp.dot(lhs_ref[:, :512], a_ref[j % 2, i], preferred_element_type=F32)
                part += jnp.dot(lhs_ref[:, 512:], b_ref[i % 2, j], preferred_element_type=F32)
                low = pl.multiple_of((d % 2) * 256, 256)
                out_ref[s // 4, s % 4, :, pl.ds(low, 256)] = part.astype(BF16)

    piece = pl.BlockSpec((2, 4, 512, 256), lambda i, e, w, s: (0, 0, 0, 0))
    return call(
        kernel,
        "weight_grad_out",
        (1,),
        3,
        [piece] * 4 + [pl.BlockSpec((16, 1, BLOCK, 256), lambda i, e, w, s: (0, 0, 0, 0))],
        pl.BlockSpec((2, 4, 256, 512), lambda i, e, w, s: (0, 0, 3, 0)),
        jax.ShapeDtypeStruct((2, 4, 1024, 512), BF16),
        [pltpu.VMEM((256, 1024), BF16)],
        2 * 1024 * 4096 * 256,
        2 * (1024 * 4096 + 16 * BLOCK * 256 + 4096 * 256),
    )(entry, where, place, *half_a, *half_b, home)


def to_seq(array):
    return lax.all_to_all(array, "seq", split_axis=0, concat_axis=0, tiled=True)


def shards(tokens, weights, grad_output, cluster, slot, pattern):
    block_count = cluster.shape[0]
    entries = 16
    head = lax.axis_index("head")
    seq = lax.axis_index("seq")
    y, z = head // 4, head % 4
    core = seq % 2

    def order(side):
        return jnp.stack([0 * side, 1 + 2 * side, 3 - 2 * side, 2 + 0 * side]).astype(jnp.int32)

    mine = order(core)
    where = ((y ^ mine)[:, None] * 4 + (z ^ mine)[None, :]).reshape(16)
    owner = jnp.arange(8, dtype=jnp.int32)
    step = (owner // 2) ^ (seq // 2)
    near = jnp.where(owner % 2 == 0, 1, 3)
    along = jnp.where(step == 0, 0, jnp.where(step == near, 1, jnp.where(step == 2, 3, 2)))
    place = ((owner % 2) ^ core) * 4 + along

    same_owner = cluster[:, None] == cluster[None, :]
    before = jnp.arange(block_count)[None, :] < jnp.arange(block_count)[:, None]
    block_rank = jnp.sum((same_owner & before).astype(jnp.int32), axis=1)
    home_entry = cluster * CAP + block_rank
    picker = home_entry[:, None] == jnp.arange(entries, dtype=jnp.int32)[None, :]
    slot_tags = (jnp.sum(jnp.where(picker, slot[:, None] + 1, 0), axis=0) - 1).reshape(8, CAP)
    tags_in = to_seq(slot_tags).reshape(entries)
    arranger = jnp.arange(CB, dtype=jnp.int32)[:, None] == tags_in[None, :]
    slot_entry = jnp.sum(
        jnp.where(arranger, jnp.arange(entries, dtype=jnp.int32)[None, :], 0), axis=1
    )
    pattern = pattern.reshape(CB * CB)

    half_a = gather_plane(grad_output[:512], "y", "z")
    half_b = gather_plane(grad_output[512:], "z", "y")

    flat = weights.reshape(weights.shape[0], 4 * weights.shape[2])
    qkv = to_seq(project(home_entry, tokens, flat))
    attention = attend_forward(slot_entry, pattern, qkv)
    attention = to_seq(attention).reshape(16, 1, BLOCK, 256)

    grad_attn = to_seq(attn_cotangent(home_entry, where, half_a, half_b, flat))

    def summed(home, count, column):
        far_a, far_b = output_parts(home_entry, where, home, flat, count, column, 1)
        near_a, near_b = output_parts(home_entry, where, home, flat, count, column, 0)
        sum_a = scatter_plane(near_a, far_a, "y", "z")
        sum_b = scatter_plane(near_b, far_b, "z", "y")
        return jnp.concatenate([sum_a, sum_b], axis=0)

    layer_out = summed(attention, 1, 3)
    grad_w = weight_grad_out(home_entry, where, place, half_a, half_b, attention)
    grads = to_seq(attend_backward(slot_entry, pattern, qkv, grad_attn))
    grad_tokens = summed(grads, 3, 0)
    grad_w = scatter_seq(weight_grad_qkv(home_entry, place, tokens, grads, grad_w))
    grad_weights = grad_w.T.reshape(512, 4, 256)
    return (layer_out, grad_tokens, grad_weights)


def solution(mesh):
    in_specs = (
        P("seq", None),
        P(None, None, "head"),
        P("seq", "head"),
        P("seq"),
        P("seq"),
        P("seq", None, None),
    )
    out_specs = (P("seq", "head"), P("seq", "head"), P("seq", None, "head"))
    return jax.shard_map(shards, mesh=mesh, in_specs=in_specs, out_specs=out_specs, check_vma=False)
```
